256 devices in a mesh: section: 8 (over x, z_lo), tensor: 32 (over z_hi, y, core).
Axes of the slice: x: 4, y: 4, z: 8 (z_hi: 4, z_lo: 2; z = z_hi * 2 + z_lo), core: 2. Of those that a mesh axis runs over, the one named last changes fastest.
Arguments:
- encoder_out: bfloat16 [1024, 4096], P('section', 'tensor'), may hold values from -6 to 6
- decoder_in: bfloat16 [8, 256, 4096], P('section', 'tensor'), may hold values from -40 to 40
- grad_output: bfloat16 [8, 256, 4096], P('section', 'tensor'), may hold values from -24 to 24
- query_weight: bfloat16 [8, 4096, 4096], P('section', None, 'tensor'), may hold values from -0.09375 to 0.09375
- key_weight: bfloat16 [8, 4096, 4096], P('section', None, 'tensor'), may hold values from -0.09375 to 0.09375
- value_weight: bfloat16 [8, 4096, 4096], P('section', None, 'tensor'), may hold values from -0.09375 to 0.09375
- out_weight: bfloat16 [8, 4096, 4096], P('section', 'tensor'), may hold values from -0.09375 to 0.09375
- head_scale: float32 [8, 64], P('section', 'tensor'), may hold values from 0.5 to 6
Outputs:
- encoder_grad: bfloat16 [1024, 4096], P('section', 'tensor')
- decoder_grad: bfloat16 [8, 256, 4096], P('section', 'tensor')
- query_weight_grad: bfloat16 [8, 4096, 4096], P('section', None, 'tensor')
- key_weight_grad: bfloat16 [8, 4096, 4096], P('section', None, 'tensor')
- value_weight_grad: bfloat16 [8, 4096, 4096], P('section', None, 'tensor')
- out_weight_grad: bfloat16 [8, 4096, 4096], P('section', 'tensor')
The draws below stay inside these ranges and needn't reach their ends.
All inputs are finite; a program needn't handle non-finite values.
Results may differ from the reference program's by a relative error of at most 0.025.
The reference program's roundings to bfloat16 on the way count: a program that leaves them out, or rounds other values in their place, can miss the bound.
Values may be sent and summed in bfloat16 or wider, within the bound.
No kernel may reach another device: no remote copies, remote signals or barrier semaphores. Data moves between devices by JAX's collectives and lax.ppermute only.
A program may use at most 128 MiB of HBM per device.

```python
import math
import jax
import jax.numpy as jnp
from jax import lax

D = 4096
HEADS = 64
HD = 64
SEQS = 2
ENC = 512
TGT = 128
LAYERS = 8
ENC_TOK = 1024
DEC_TOK = 256
N_TENSOR = 32


def draw_decoder_in(key, part):
    base_key, row_key, column_key = jax.random.split(key, 3)
    full_shape = (LAYERS, DEC_TOK, D)
    row_scale = jnp.exp(jax.random.uniform(row_key, (LAYERS, DEC_TOK, 1), jnp.float32, math.log(0.5), math.log(5.0)))
    column_scale = jnp.exp(jax.random.uniform(column_key, (1, 1, D), jnp.float32, math.log(0.5), math.log(2.0)))
    values = jnp.clip(jax.random.normal(base_key, full_shape, jnp.float32), -4.0, 4.0)
    return (values * row_scale * column_scale).astype(jnp.bfloat16)


def draw_head_scale(key, part):
    ceiling = 4.0
    return jnp.exp(jax.random.uniform(key, (LAYERS, HEADS), jnp.float32, math.log(0.5), math.log(ceiling)))


def block_levels(own_key, dims, cuts, smallest, largest):
    factor_of, own = 1.0, jax.random.fold_in(own_key, 6)
    for position, blocks in cuts:
        steps = jnp.exp(jax.random.uniform(jax.random.fold_in(own, position), (blocks,), jnp.float32, smallest / len(cuts), largest / len(cuts)))
        factor_of = factor_of * jnp.repeat(steps, dims[position] // blocks).reshape([-1 if axis == position else 1 for axis in range(len(dims))])
    return factor_of


def noise(key, shape, spread, limit, shards=(), held_as=jnp.bfloat16):
    values = spread * jax.random.normal(key, shape, jnp.float32)
    if shards:
        values = values * block_levels(key, shape, shards, -0.22, 0.18)
    return jnp.clip(values, -limit, limit).astype(held_as)


def setup_inputs(seed: int = 0) -> dict:
    keys = jax.random.split(jax.random.key(seed), 9)
    return {
        "encoder_out": noise(keys[0], (ENC_TOK, D), 1.0, 6.0, ((0, 8), (1, 32))),
        "decoder_in": draw_decoder_in(jax.random.fold_in(keys[8], 71), 0),
        "grad_output": noise(keys[2], (LAYERS, DEC_TOK, D), 4.0, 24.0, ((0, 8), (1, 32))),
        "query_weight": noise(keys[3], (LAYERS, D, HEADS * HD), D ** -0.5, 0.09375, ((0, 8), (2, 32))),
        "key_weight": noise(keys[4], (LAYERS, D, HEADS * HD), D ** -0.5, 0.09375, ((0, 8), (2, 32))),
        "value_weight": noise(keys[5], (LAYERS, D, HEADS * HD), D ** -0.5, 0.09375, ((0, 8), (2, 32))),
        "out_weight": noise(keys[6], (LAYERS, HEADS * HD, D), (HEADS * HD) ** -0.5, 0.09375, ((0, 8), (1, 32))),
        "head_scale": draw_head_scale(jax.random.fold_in(keys[8], 71), 0),
    }


EPSILON = 1e-06

def by_group(matrix, group_width):
    return matrix.reshape(matrix.shape[0], N_TENSOR, group_width).transpose(1, 0, 2)

def cross_layer(encoder_out, layer_item):
    decoder_in, grad_output, query_weight, key_weight, value_weight, out_weight, head_scale = layer_item
    inner_width = HEADS * HD
    floated = decoder_in.astype(jnp.float32)
    inv_rms = lax.rsqrt(lax.optimization_barrier(jnp.mean(floated * floated, axis=-1, keepdims=True)) + EPSILON)
    normed_full = floated * inv_rms
    normed = normed_full.astype(jnp.bfloat16)
    query_rows = jnp.dot(normed, query_weight, preferred_element_type=jnp.float32).astype(jnp.bfloat16)
    key_rows = jnp.dot(encoder_out, key_weight, preferred_element_type=jnp.float32).astype(jnp.bfloat16)
    value_rows = jnp.dot(encoder_out, value_weight, preferred_element_type=jnp.float32).astype(jnp.bfloat16)
    query_four = lax.optimization_barrier(query_rows).reshape(SEQS, TGT, HEADS, HD).astype(jnp.float32)
    key_four = lax.optimization_barrier(key_rows).reshape(SEQS, ENC, HEADS, HD).astype(jnp.float32)
    value_four = lax.optimization_barrier(value_rows).reshape(SEQS, ENC, HEADS, HD).astype(jnp.float32)
    factor = (head_scale / math.sqrt(HD))[None, :, None, None]
    scores = jnp.einsum('bthc,bshc->bhts', query_four, key_four) * factor
    softmaxed = jax.nn.softmax(scores, axis=-1)
    weights = lax.optimization_barrier(softmaxed.astype(jnp.bfloat16)).astype(jnp.float32)
    attended = jnp.einsum('bhts,bshc->bthc', weights, value_four).astype(jnp.bfloat16).reshape(DEC_TOK, inner_width)
    out_weight_grad = jnp.dot(attended.T, grad_output, preferred_element_type=jnp.float32).astype(jnp.bfloat16)
    grad_attended = jnp.dot(grad_output, out_weight.T, preferred_element_type=jnp.float32).astype(jnp.bfloat16)
    grad_four = lax.optimization_barrier(grad_attended).reshape(SEQS, TGT, HEADS, HD).astype(jnp.float32)
    grad_weights = jnp.einsum('bthc,bshc->bhts', grad_four, value_four)
    grad_value = jnp.einsum('bhts,bthc->bshc', weights, grad_four).astype(jnp.bfloat16).reshape(ENC_TOK, inner_width)
    grad_scores = softmaxed * (grad_weights - lax.optimization_barrier(jnp.sum(softmaxed * grad_weights, axis=-1, keepdims=True)))
    scaled = lax.optimization_barrier((grad_scores * factor).astype(jnp.bfloat16)).astype(jnp.float32)
    grad_query = jnp.einsum('bhts,bshc->bthc', scaled, key_four).astype(jnp.bfloat16).reshape(DEC_TOK, inner_width)
    grad_key = jnp.einsum('bhts,bthc->bshc', scaled, query_four).astype(jnp.bfloat16).reshape(ENC_TOK, inner_width)
    query_weight_grad = jnp.dot(normed.T, grad_query, preferred_element_type=jnp.float32).astype(jnp.bfloat16)
    key_weight_grad = jnp.dot(encoder_out.T, grad_key, preferred_element_type=jnp.float32).astype(jnp.bfloat16)
    value_weight_grad = jnp.dot(encoder_out.T, grad_value, preferred_element_type=jnp.float32).astype(jnp.bfloat16)
    grad_normed = jnp.dot(grad_query, query_weight.T, preferred_element_type=jnp.float32)
    decoder_grad = ((grad_normed - normed_full * lax.optimization_barrier(jnp.mean(grad_normed * normed_full, axis=-1, keepdims=True))) * inv_rms).astype(jnp.bfloat16)
    group_width = inner_width // N_TENSOR
    pieces = (by_group(grad_key, group_width), by_group(key_weight, group_width), by_group(grad_value, group_width), by_group(value_weight, group_width))

    def group_term(running, group_pieces):
        key_part, wkey_part, value_part, wvalue_part = group_pieces
        term_sum = jnp.dot(key_part, wkey_part.T, preferred_element_type=jnp.float32) + jnp.dot(value_part, wvalue_part.T, preferred_element_type=jnp.float32)
        rounded = lax.optimization_barrier(term_sum.astype(jnp.bfloat16))
        return (running + rounded.astype(jnp.float32), None)
    encoder_term = lax.scan(group_term, jnp.zeros((ENC_TOK, D), jnp.float32), pieces)[0]
    return (encoder_term, (decoder_grad, query_weight_grad, key_weight_grad, value_weight_grad, out_weight_grad))

def reference(encoder_out, decoder_in, grad_output, query_weight, key_weight, value_weight, out_weight, head_scale):

    def layer_step(encoder_total, layer_item):
        encoder_term, layer_grads = cross_layer(encoder_out, layer_item)
        return (encoder_total + encoder_term, layer_grads)
    start_total = jnp.zeros((ENC_TOK, D), jnp.float32)
    encoder_total, stacked = lax.scan(layer_step, start_total, (decoder_in, grad_output, query_weight, key_weight, value_weight, out_weight, head_scale))
    decoder_grad, query_weight_grad, key_weight_grad, value_weight_grad, out_weight_grad = stacked
    return (encoder_total.astype(jnp.bfloat16), decoder_grad, query_weight_grad, key_weight_grad, value_weight_grad, out_weight_grad)
```

```python
import math

import jax
import jax.numpy as jnp
from jax import lax
from jax.sharding import PartitionSpec as P

HD = 64
SEQS = 2
EPSILON = 1e-06
AXES = ("section", "tensor")
X, Z, Y, CORES = 4, 8, 4, 2
ROWS_BY_ROWS = (((0,), (0,)), ((), ()))
COLS_BY_COLS = (((1,), (1,)), ((), ()))


def product(first_matrix, second_matrix, contracted):
    return lax.dot_general(
        first_matrix, second_matrix, contracted, preferred_element_type=jnp.float32
    )


def flat(x, y, z, core):
    x, y, z, core = x % X, y % Y, z % Z, core % CORES
    return (x * 2 + z % 2) * 32 + (z // 2) * 8 + y * 2 + core


def move(value, x=0, y=0, z=0, core=0):
    pairs = [
        (flat(i, j, k, m), flat(i + x, j + y, k + z, m + core))
        for i in range(X)
        for j in range(Y)
        for k in range(Z)
        for m in range(CORES)
    ]
    return lax.ppermute(value, AXES, pairs)


def at(stacked, index):
    return lax.dynamic_index_in_dim(stacked, index, 0, keepdims=False)


def absolute(relative, position):
    count = relative.shape[0]
    doubled = jnp.concatenate([relative, relative], axis=0)
    return lax.dynamic_slice_in_dim(doubled, (count - position) % count, count, 0)


def ordered(own, other, core):
    return jnp.where(core == 0, jnp.stack([own, other]), jnp.stack([other, own]))


def gather_ring(own, **axis):
    (name, stride), = axis.items()
    half = own.shape[0] // 2
    behind = move(own, **{name: stride})
    ahead = move(own, **{name: -stride})
    far_low = move(behind[:half], **{name: stride})
    far_high = move(ahead[half:], **{name: -stride})
    return own, ahead, jnp.concatenate([far_low, far_high], axis=0), behind


def scatter_ring(blocks, **axis):
    (name, stride), = axis.items()
    half = blocks[0].shape[0] // 2
    low = move(blocks[2][:half], **{name: stride})
    high = move(blocks[2][half:], **{name: -stride})
    up = jnp.concatenate([add(blocks[1][:half], low), blocks[1][half:]], axis=0)
    down = jnp.concatenate([blocks[3][:half], add(blocks[3][half:], high)], axis=0)
    from_below = move(up, **{name: stride})
    from_above = move(down, **{name: -stride})
    return add(blocks[0], from_below, from_above)


def add(*terms):
    total = terms[0].astype(jnp.float32)
    for term in terms[1:]:
        total = total + term.astype(jnp.float32)
    return total.astype(jnp.bfloat16)


def per_device(
    encoder_out,
    decoder_in,
    grad_output,
    query_weight,
    key_weight,
    value_weight,
    out_weight,
    head_scale,
):
    section, tensor = lax.axis_index("section"), lax.axis_index("tensor")
    x, z_hi, y, core = section // 2, tensor // 8, (tensor // 2) % 4, tensor % 2
    z = z_hi * 2 + section % 2
    local_query = query_weight[0]
    local_key = key_weight[0]
    local_value = value_weight[0]
    local_out = out_weight[0]
    width = encoder_out.shape[1] * 32
    tokens = encoder_out.shape[0]
    half = tokens // 2
    rows = decoder_in.shape[1]
    cols = local_query.shape[1]
    local_heads = cols // HD

    floated = decoder_in[0].astype(jnp.float32)
    inv_rms = lax.rsqrt(jnp.mean(floated * floated, axis=-1, keepdims=True) + EPSILON)
    normed_full = floated * inv_rms
    normed = normed_full.astype(jnp.bfloat16)
    mine = jnp.where(core == 0, normed, grad_output[0])
    theirs = jnp.where(core == 0, grad_output[0], normed)
    block = ordered(mine, move(theirs, core=1), core).reshape(2 * rows, width)

    halves = encoder_out.reshape(2, half, tokens)
    piece = jnp.concatenate(
        list(ordered(at(halves, core), move(at(halves, 1 - core), core=1), core)), axis=1
    )
    places = [piece] + [move(piece, z=-k) for k in range(1, Z)]
    stack = absolute(jnp.stack(places), z)

    parts = jnp.stack([block[:, : width // 2], block[:, width // 2 :]])
    parts = jnp.stack(gather_ring(parts, z=2))
    parts = absolute(parts, z_hi)
    parts = parts.transpose(0, 2, 1, 3).reshape(4, 2 * rows, width)
    dec_mine = gather_ring(parts, y=1)

    stack = jnp.stack(gather_ring(stack, y=1))
    stack = absolute(stack, y).reshape(4, 4, 2, half, 2 * tokens)
    own_piece = stack.transpose(2, 3, 1, 0, 4).reshape(2, half, width)
    enc_mine = gather_ring(own_piece, x=1)

    sib_key = move(local_key, core=1)
    sib_value = move(local_value, core=1)
    query_halves = local_query.reshape(2, width // 2, cols)
    sib_query = move(at(query_halves, 1 - core), core=1)

    dec_theirs = [move(part, core=1) for part in dec_mine]
    enc_theirs = [move(part, core=1) for part in enc_mine]
    dec_rows = 4 * 4 * 2 * rows
    mine_all = jnp.concatenate(dec_mine, axis=0).reshape(dec_rows, width)
    theirs_all = jnp.concatenate(dec_theirs, axis=0).reshape(dec_rows, width)
    normed_all = jnp.where(core == 0, mine_all, theirs_all)
    cotangent = jnp.where(core == 0, theirs_all, mine_all)
    encoder = jnp.stack(
        [part for pair in zip(enc_mine, enc_theirs) for part in pair]
    ).reshape(-1, width)

    def to_sequences(values):
        return (
            values.reshape(4, 4, 2 * rows, cols).transpose(1, 0, 2, 3).reshape(SEQS, -1, local_heads, HD)
        )

    def from_sequences(values):
        return (
            values.reshape(4, 4, 2 * rows, cols).transpose(1, 0, 2, 3).reshape(dec_rows, cols)
        )

    def to_absolute(values):
        return absolute(values.reshape(4, -1, cols), x).reshape(SEQS, -1, local_heads, HD)

    def to_relative(values):
        return absolute(values.reshape(4, -1, cols), (4 - x) % 4)

    query_rows = jnp.dot(normed_all, local_query, preferred_element_type=jnp.float32).astype(
        jnp.bfloat16
    )
    key_rows = jnp.dot(encoder, local_key, preferred_element_type=jnp.float32).astype(jnp.bfloat16)
    value_rows = jnp.dot(encoder, local_value, preferred_element_type=jnp.float32).astype(
        jnp.bfloat16
    )
    grad_attended = product(cotangent, local_out, COLS_BY_COLS).astype(jnp.bfloat16)
    query_four = to_sequences(query_rows)
    grad_four = to_sequences(grad_attended)
    key_four = to_absolute(key_rows)
    value_four = to_absolute(value_rows)
    factor = (head_scale[0] / math.sqrt(HD))[None, :, None, None]
    scores = (
        jnp.einsum("bthc,bshc->bhts", query_four, key_four, preferred_element_type=jnp.float32)
        * factor
    )
    softmaxed = jax.nn.softmax(scores, axis=-1)
    weights = softmaxed.astype(jnp.bfloat16)
    attended = from_sequences(
        jnp.einsum(
            "bhts,bshc->bthc", weights, value_four, preferred_element_type=jnp.float32
        ).astype(jnp.bfloat16)
    )
    out_weight_grad = product(attended, cotangent, ROWS_BY_ROWS).astype(jnp.bfloat16)
    grad_weights = jnp.einsum(
        "bthc,bshc->bhts", grad_four, value_four, preferred_element_type=jnp.float32
    )
    grad_value = to_relative(
        jnp.einsum(
            "bhts,bthc->bshc", weights, grad_four, preferred_element_type=jnp.float32
        ).astype(jnp.bfloat16)
    )
    grad_scores = softmaxed * (
        grad_weights - jnp.sum(softmaxed * grad_weights, axis=-1, keepdims=True)
    )
    scaled = (grad_scores * factor).astype(jnp.bfloat16)
    grad_query = from_sequences(
        jnp.einsum(
            "bhts,bshc->bthc", scaled, key_four, preferred_element_type=jnp.float32
        ).astype(jnp.bfloat16)
    )
    grad_key = to_relative(
        jnp.einsum(
            "bhts,bthc->bshc", scaled, query_four, preferred_element_type=jnp.float32
        ).astype(jnp.bfloat16)
    )

    both = jnp.stack([grad_key, grad_value]).reshape(2, 4, 2, tokens, cols)
    sib_both = move(both[:, :, 1], core=1)
    joined = jnp.concatenate(
        [both[0, :, 0], both[1, :, 0], sib_both[0], sib_both[1]], axis=-1
    )
    joined_weight = jnp.concatenate([local_key, local_value, sib_key, sib_value], axis=1)

    def term(k):
        return (
            product(joined[k], joined_weight, COLS_BY_COLS)
            .astype(jnp.bfloat16)
            .reshape(2, half, width)
        )

    summed = scatter_ring([term(k) for k in range(4)], x=1)
    summed = summed.reshape(2, half, 4, 4, 2 * tokens).transpose(3, 2, 0, 1, 4)
    summed = summed.reshape(4, Z, half, 2 * tokens)
    summed = scatter_ring([at(summed, (y + k) % 4) for k in range(4)], y=1)
    arrived = [at(summed, z)] + [move(at(summed, (z + k) % Z), z=k) for k in range(1, Z)]
    final = add(*arrived).reshape(half, 2, tokens).transpose(1, 0, 2)
    encoder_grad = ordered(
        at(final, core), move(at(final, 1 - core), core=1), core
    ).reshape(tokens, tokens)

    sib_grad_query = move(grad_query, core=1)
    query_joined = jnp.concatenate([grad_query, sib_grad_query], axis=1)
    query_joined_weight = jnp.concatenate([at(query_halves, core), sib_query], axis=1)
    partial = (
        product(query_joined, query_joined_weight, COLS_BY_COLS)
        .astype(jnp.bfloat16)
        .reshape(4, 4, 2 * rows, width // 2)
    )
    rows_summed = scatter_ring(list(partial), y=1)
    arrived = [at(rows_summed, z_hi)] + [
        move(at(rows_summed, (z_hi + k) % 4), z=2 * k) for k in range(1, 4)
    ]
    total = sum(part.astype(jnp.float32) for part in arrived).reshape(2, rows, width // 2)
    grad_normed = jnp.concatenate(
        list(ordered(at(total, core), move(at(total, 1 - core), core=1), core)), axis=1
    )
    decoder_grad = (
        (grad_normed - normed_full * jnp.mean(grad_normed * normed_full, axis=-1, keepdims=True))
        * inv_rms
    ).astype(jnp.bfloat16)

    query_weight_grad = product(normed_all, grad_query, ROWS_BY_ROWS).astype(jnp.bfloat16)
    key_weight_grad = product(encoder, grad_key.reshape(-1, cols), ROWS_BY_ROWS).astype(
        jnp.bfloat16
    )
    value_weight_grad = product(encoder, grad_value.reshape(-1, cols), ROWS_BY_ROWS).astype(
        jnp.bfloat16
    )
    return (
        encoder_grad,
        decoder_grad[None],
        query_weight_grad[None],
        key_weight_grad[None],
        value_weight_grad[None],
        out_weight_grad[None],
    )


def solution(mesh):
    placed = (
        P("section", "tensor"),
        P("section", "tensor", None),
        P("section", "tensor", None),
        P("section", None, "tensor"),
        P("section", None, "tensor"),
        P("section", None, "tensor"),
        P("section", "tensor", None),
        P("section", "tensor"),
    )
    return jax.shard_map(
        per_device,
        mesh=mesh,
        in_specs=placed,
        out_specs=(
            P("section", "tensor"),
            P("section", "tensor", None),
            P("section", None, "tensor"),
            P("section", None, "tensor"),
            P("section", None, "tensor"),
            P("section", "tensor", None),
        ),
        check_vma=False,
    )
```

```python
import math

import jax
import jax.numpy as jnp
from jax import lax
from jax.experimental import pallas as pl
from jax.experimental.pallas import tpu as pltpu
from jax.sharding import Mesh, PartitionSpec as P

HD = 64
SEQS = 2
EPSILON = 1e-06
AXES = ("x", "z_lo", "z_hi", "y", "core")
X, Z, Y, CORES = 4, 8, 4, 2
GROUPS = 16
ROWS_BY_ROWS = (((0,), (0,)), ((), ()))
COLS_BY_COLS = (((1,), (1,)), ((), ()))
COLS_BY_ROWS = (((1,), (0,)), ((), ()))
IN_SMEM = pl.BlockSpec(memory_space=pltpu.SMEM)
IN_VMEM = pl.BlockSpec(memory_space=pltpu.VMEM)


def product(first_matrix, second_matrix, contracted):
    return lax.dot_general(
        first_matrix, second_matrix, contracted, preferred_element_type=jnp.float32
    )


def to_sibling(value):
    return lax.ppermute(value, "core", [(0, 1), (1, 0)])


def at(stacked, index):
    return lax.dynamic_index_in_dim(stacked, index, 0, keepdims=False)


def ordered(own, other, core):
    return jnp.where(core == 0, jnp.stack([own, other]), jnp.stack([other, own]))


def from_all(value, axis, count):
    copies = jnp.broadcast_to(value[None], (count,) + value.shape)
    return lax.all_to_all(copies, axis, 0, 0, tiled=True)


def sum_to_owner(blocks, axis):
    return add(lax.all_to_all(blocks, axis, 0, 0, tiled=True))


def add(*terms):
    total = terms[0].astype(jnp.float32)
    if len(terms) == 1:
        return jnp.sum(total, axis=0)
    for term in terms[1:]:
        total = total + term.astype(jnp.float32)
    return total


def step(value, axis, distance):
    return lax.ppermute(value, axis, [(i, (i + distance) % 4) for i in range(4)])


def gather_ring(own, axis):
    half = own.shape[0] // 2
    behind = step(own, axis, 1)
    ahead = step(own, axis, -1)
    far_low = step(behind[:half], axis, 1)
    far_high = step(ahead[half:], axis, -1)
    return jnp.stack([own, ahead, jnp.concatenate([far_low, far_high], axis=0), behind])


def scatter_ring(blocks, axis):
    half = blocks.shape[1] // 2

    def joined(own, received):
        return add(own, received).astype(own.dtype)

    low = step(blocks[2, :half], axis, 1)
    high = step(blocks[2, half:], axis, -1)
    up = jnp.concatenate([joined(blocks[1, :half], low), blocks[1, half:]], axis=0)
    down = jnp.concatenate([blocks[3, :half], joined(blocks[3, half:], high)], axis=0)
    return add(blocks[0], step(up, axis, 1), step(down, axis, -1))


def rotated(blocks, shift):
    doubled = jnp.concatenate([blocks, blocks], axis=0)
    return lax.dynamic_slice_in_dim(doubled, shift, blocks.shape[0], 0)


def group_spec(rows, features, count):
    if count == Y:
        return pl.BlockSpec((X, Y, 1, 2, rows, features), lambda i: (0, 0, i, 0, 0, 0))
    return pl.BlockSpec(
        (X, 1, 1, 2, rows, features), lambda i: (0, lax.rem(i, 4), lax.div(i, 4), 0, 0, 0)
    )


def project_kernel(encoder_ref, weight_ref, own_ref, sibling_ref, total_ref):
    index = pl.program_id(0)
    features = encoder_ref.shape[-1]
    encoder = jnp.concatenate(
        [encoder_ref[:, y].reshape(-1, features) for y in range(Y)], axis=-1
    )
    partial = product(encoder, weight_ref[0], COLS_BY_ROWS)

    @pl.when(index == 0)
    def _():
        total_ref[...] = partial

    @pl.when(index > 0)
    def _():
        total_ref[...] += partial

    @pl.when(index == Z // 2 - 1)
    def _():
        cols = own_ref.shape[-1]
        rounded = total_ref[...].astype(jnp.bfloat16)
        own_ref[...] = rounded[:, :cols].reshape(own_ref.shape)
        sibling_ref[...] = rounded[:, cols:].reshape(own_ref.shape)


def project(encoder, weight):
    rows, features = encoder.shape[-2:]
    cols = weight.shape[-1]
    out = jax.ShapeDtypeStruct((X, 2 * rows, cols // 2), jnp.bfloat16)
    whole = pl.BlockSpec(out.shape, lambda i: (0, 0, 0))
    return pl.pallas_call(
        project_kernel,
        grid=(Z // 2,),
        out_shape=[out, out],
        in_specs=[
            group_spec(rows, features, Y),
            pl.BlockSpec((1, Y * features, cols), lambda i: (i, 0, 0)),
        ],
        out_specs=[whole, whole],
        scratch_shapes=[pltpu.VMEM((X * 2 * rows, cols), jnp.float32)],
        compiler_params=pltpu.CompilerParams(vmem_limit_bytes=20 << 20),
        cost_estimate=pl.CostEstimate(
            flops=2_200_000_000, bytes_accessed=9_000_000, transcendentals=0
        ),
    )(encoder, weight.reshape(Z // 2, Y * features, cols))


def term_kernel(own_ref, other_ref, weight_ref, out_ref):
    cols = own_ref.shape[-1]
    joined = jnp.concatenate(
        [ref[...].reshape(-1, cols) for ref in (own_ref, other_ref)], axis=-1
    )
    terms = product(joined, weight_ref[0], COLS_BY_COLS).astype(jnp.bfloat16)
    features = out_ref.shape[-1]
    shape = (X,) + out_ref.shape[2:]
    for y in range(Y):
        out_ref[:, y] = terms[:, y * features : (y + 1) * features].reshape(shape)


def encoder_terms(own, other, weight):
    rows, cols = own.shape[1] // 2, weight.shape[-1]
    features = weight.shape[0] // GROUPS
    return pl.pallas_call(
        term_kernel,
        grid=(Z // 2,),
        out_shape=jax.ShapeDtypeStruct((X, Y, Z // 2, 2, rows, features), jnp.bfloat16),
        in_specs=[pl.BlockSpec(own.shape, lambda i: (0, 0, 0))] * 2
        + [pl.BlockSpec((1, Y * features, cols), lambda i: (i, 0, 0))],
        out_specs=group_spec(rows, features, Y),
        compiler_params=pltpu.CompilerParams(vmem_limit_bytes=20 << 20),
        cost_estimate=pl.CostEstimate(
            flops=2_200_000_000, bytes_accessed=9_000_000, transcendentals=0
        ),
    )(own, other, weight.reshape(Z // 2, Y * features, cols))


def weight_grad_kernel(encoder_ref, encoder_other_ref, own_ref, other_ref, key_ref, value_ref):
    features = encoder_ref.shape[-1]
    cols = key_ref.shape[-1]
    tokens = jnp.concatenate(
        [ref[...].reshape(-1, features) for ref in (encoder_ref, encoder_other_ref)], axis=0
    )
    grads = jnp.concatenate(
        [ref[...].reshape(-1, 2 * cols) for ref in (own_ref, other_ref)], axis=0
    )
    both = product(tokens, grads, ROWS_BY_ROWS).astype(jnp.bfloat16)
    key_ref[...] = both[:, :cols]
    value_ref[...] = both[:, cols:]


def weight_grads(encoder, encoder_other, own, other):
    rows, features = encoder.shape[-2:]
    cols = own.shape[-1] // 2
    out = jax.ShapeDtypeStruct((GROUPS * features, cols), jnp.bfloat16)
    return pl.pallas_call(
        weight_grad_kernel,
        grid=(GROUPS,),
        out_shape=[out, out],
        in_specs=[group_spec(rows, features, 1)] * 2
        + [pl.BlockSpec(own.shape, lambda i: (0, 0, 0))] * 2,
        out_specs=[pl.BlockSpec((features, cols), lambda i: (i, 0))] * 2,
        compiler_params=pltpu.CompilerParams(vmem_limit_bytes=16 << 20),
        cost_estimate=pl.CostEstimate(
            flops=2_200_000_000, bytes_accessed=11_000_000, transcendentals=0
        ),
    )(encoder, encoder_other, own, other)


def attention_kernel(
    scale_ref,
    query_ref,
    grad_ref,
    own_ref,
    other_ref,
    attended_ref,
    grad_query_ref,
    grad_own_ref,
    grad_other_ref,
):
    rows = query_ref.shape[0] // SEQS
    cols = own_ref.shape[-1]
    places = X // SEQS
    for seq in range(SEQS):
        of_x = slice(seq * places, (seq + 1) * places)
        of_rows = slice(seq * rows, (seq + 1) * rows)
        kv = jnp.concatenate(
            [ref[of_x].reshape(-1, cols) for ref in (own_ref, other_ref)], axis=0
        )
        attended, grad_query, grad_key, grad_value = [], [], [], []
        for head in range(2):
            lanes = slice(head * HD, (head + 1) * HD)
            query, grad = query_ref[of_rows, lanes], grad_ref[of_rows, lanes]
            key, value = kv[:, : 2 * HD][:, lanes], kv[:, 2 * HD :][:, lanes]
            factor = scale_ref[0, head] * (1.0 / math.sqrt(HD))
            scores = product(query, key, COLS_BY_COLS) * factor
            powers = jnp.exp(scores - jnp.max(scores, axis=-1, keepdims=True))
            softmaxed = powers / jnp.sum(powers, axis=-1, keepdims=True)
            weights = softmaxed.astype(jnp.bfloat16)
            grad_weights = product(grad, value, COLS_BY_COLS)
            grad_scores = softmaxed * (
                grad_weights - jnp.sum(softmaxed * grad_weights, axis=-1, keepdims=True)
            )
            scaled = (grad_scores * factor).astype(jnp.bfloat16)
            attended.append(product(weights, value, COLS_BY_ROWS))
            grad_query.append(product(scaled, key, COLS_BY_ROWS))
            grad_key.append(product(scaled, query, ROWS_BY_ROWS))
            grad_value.append(product(weights, grad, ROWS_BY_ROWS))

        def joined(parts):
            return jnp.concatenate(parts, axis=-1).astype(jnp.bfloat16)

        attended_ref[of_rows] = joined(attended)
        grad_query_ref[of_rows] = joined(grad_query)
        grad_kv = joined(grad_key + grad_value)
        half = grad_kv.shape[0] // 2
        shape = (places,) + own_ref.shape[1:]
        grad_own_ref[of_x] = grad_kv[:half].reshape(shape)
        grad_other_ref[of_x] = grad_kv[half:].reshape(shape)


def attention(scale, query, grad, own, other):
    rows = jax.ShapeDtypeStruct(query.shape, query.dtype)
    tokens = jax.ShapeDtypeStruct(own.shape, own.dtype)
    return pl.pallas_call(
        attention_kernel,
        out_shape=[rows, rows, tokens, tokens],
        in_specs=[IN_SMEM] + [IN_VMEM] * 4,
        out_specs=[IN_VMEM] * 4,
        compiler_params=pltpu.CompilerParams(vmem_limit_bytes=24 << 20),
        cost_estimate=pl.CostEstimate(
            flops=210_000_000, bytes_accessed=1_500_000, transcendentals=270_000
        ),
    )(scale, query, grad, own, other)


def per_device(
    encoder_out,
    decoder_in,
    grad_output,
    query_weight,
    key_weight,
    value_weight,
    out_weight,
    head_scale,
):
    core, z_hi = lax.axis_index("core"), lax.axis_index("z_hi")
    local_query = query_weight[0]
    local_out = out_weight[0]
    tokens = encoder_out.shape[0]
    half, features = tokens // 2, 2 * tokens
    rows, width = decoder_in.shape[1:]
    cols = local_query.shape[1]
    dec_rows = Z // 2 * Y * CORES * rows

    floated = decoder_in[0].astype(jnp.float32)
    inv_rms = lax.rsqrt(jnp.mean(floated * floated, axis=-1, keepdims=True) + EPSILON)
    normed_full = floated * inv_rms
    normed = normed_full.astype(jnp.bfloat16)
    mine = jnp.where(core == 0, normed, grad_output[0])
    theirs = jnp.where(core == 0, grad_output[0], normed)
    block = ordered(mine, to_sibling(theirs), core).reshape(2 * rows, width)

    halves = encoder_out.reshape(2, half, tokens)
    piece = jnp.concatenate(
        list(ordered(at(halves, core), to_sibling(at(halves, 1 - core)), core)), axis=1
    )
    stack = from_all(piece, ("z_hi", "z_lo"), Z)
    blocks = jnp.stack([block] + [step(block, "y", -k) for k in range(1, Y)])
    stack, blocks = lax.optimization_barrier((stack, blocks))
    encoder = from_all(stack, ("x", "y"), X * Y).reshape(X, Y, Z // 2, 2, half, features)
    gathered = gather_ring(blocks, "z_hi").reshape(dec_rows, width)

    local_kv = jnp.concatenate([key_weight[0], value_weight[0]], axis=1)
    joined_kv = jnp.concatenate([local_kv, to_sibling(local_kv)], axis=1)
    query_halves = local_query.reshape(2, width // 2, cols)
    joined_query = jnp.concatenate(
        [at(query_halves, core), to_sibling(at(query_halves, 1 - core))], axis=1
    )
    out_columns = local_out.T
    row_weight = jnp.concatenate(
        [
            jnp.where(core == 0, local_query, out_columns),
            to_sibling(jnp.where(core == 0, out_columns, local_query)),
        ],
        axis=1,
    )

    made = jnp.dot(gathered, row_weight, preferred_element_type=jnp.float32).astype(jnp.bfloat16)
    by_place = (Z // 2, dec_rows // 4, -1)
    made = rotated(made.reshape(by_place), (4 - z_hi) % 4).reshape(dec_rows, -1)
    made_own, made_other = made[:, :cols], to_sibling(made[:, cols:])
    query_rows = jnp.where(core == 0, made_own, made_other)
    grad_attended = jnp.where(core == 0, made_other, made_own)
    kv_own, kv_sibling = project(encoder, joined_kv)
    attended, grad_query, grad_kv_own, grad_kv_other = attention(
        head_scale, query_rows, grad_attended, kv_own, to_sibling(kv_sibling)
    )

    grad_kv_received = to_sibling(grad_kv_other)
    attended = rotated(attended.reshape(by_place), z_hi).reshape(dec_rows, cols)
    grad_query = rotated(grad_query.reshape(by_place), z_hi).reshape(dec_rows, cols)
    terms = encoder_terms(grad_kv_own, grad_kv_received, joined_kv)
    terms, encoder, gathered, grad_query = lax.optimization_barrier(
        (terms, encoder, gathered, grad_query)
    )
    arrived = lax.all_to_all(
        terms.reshape(X * Y, Z, half, features), ("x", "y"), 0, 0, tiled=True
    )

    others = to_sibling(gathered)
    normed_all = jnp.where(core == 0, gathered, others)
    cotangent = jnp.where(core == 0, others, gathered)
    out_weight_grad = product(attended, cotangent, ROWS_BY_ROWS).astype(jnp.bfloat16)
    query_weight_grad = product(normed_all, grad_query, ROWS_BY_ROWS).astype(jnp.bfloat16)
    key_weight_grad, value_weight_grad = weight_grads(
        encoder, to_sibling(encoder), grad_kv_own, grad_kv_other
    )

    query_joined = jnp.concatenate([grad_query, to_sibling(grad_query)], axis=1)
    partial = product(query_joined, joined_query, COLS_BY_COLS).astype(jnp.bfloat16)
    partial = partial.reshape(Z // 2, Y, 2 * rows, width // 2)
    total = scatter_ring(partial, "z_hi").astype(jnp.bfloat16)

    (
        arrived,
        total,
        query_weight_grad,
        key_weight_grad,
        value_weight_grad,
        out_weight_grad,
    ) = lax.optimization_barrier(
        (
            arrived,
            total,
            query_weight_grad,
            key_weight_grad,
            value_weight_grad,
            out_weight_grad,
        )
    )
    final = sum_to_owner(add(arrived).astype(jnp.bfloat16), ("z_hi", "z_lo"))
    final = final.astype(jnp.bfloat16).reshape(half, 2, tokens).transpose(1, 0, 2)
    encoder_grad = ordered(
        at(final, core), to_sibling(at(final, 1 - core)), core
    ).reshape(tokens, tokens)

    total = add(total[0], *[step(total[k], "y", k) for k in range(1, Y)])
    total = total.reshape(2, rows, width // 2)
    grad_normed = jnp.concatenate(
        list(ordered(at(total, core), to_sibling(at(total, 1 - core)), core)), axis=1
    )
    decoder_grad = (
        (grad_normed - normed_full * jnp.mean(grad_normed * normed_full, axis=-1, keepdims=True))
        * inv_rms
    ).astype(jnp.bfloat16)

    return (
        encoder_grad,
        decoder_grad[None],
        query_weight_grad[None],
        key_weight_grad[None],
        value_weight_grad[None],
        out_weight_grad[None],
    )


def solution(mesh):
    section, tensor = AXES[:2], AXES[2:]
    placed = (
        P(section, tensor),
        P(section, tensor, None),
        P(section, tensor, None),
        P(section, None, tensor),
        P(section, None, tensor),
        P(section, None, tensor),
        P(section, tensor, None),
        P(section, tensor),
    )
    return jax.shard_map(
        per_device,
        mesh=Mesh(mesh.devices.reshape(X, 2, Z // 2, Y, CORES), AXES),
        in_specs=placed,
        out_specs=placed[:2] + placed[3:7],
        check_vma=False,
    )
```

```python
import math

import jax
import jax.numpy as jnp
from jax import lax
from jax.experimental import pallas as pl
from jax.experimental.pallas import tpu as pltpu
from jax.sharding import Mesh, PartitionSpec as P

HD = 64
SEQS = 2
EPSILON = 1e-06
AXES = ("x", "z_lo", "z_hi", "y", "core")
X, Z, Y, CORES = 4, 8, 4, 2
GROUPS = 16
ROWS_BY_ROWS = (((0,), (0,)), ((), ()))
COLS_BY_COLS = (((1,), (1,)), ((), ()))
COLS_BY_ROWS = (((1,), (0,)), ((), ()))
IN_SMEM = pl.BlockSpec(memory_space=pltpu.SMEM)
IN_VMEM = pl.BlockSpec(memory_space=pltpu.VMEM)


def product(first_matrix, second_matrix, contracted):
    return lax.dot_general(
        first_matrix, second_matrix, contracted, preferred_element_type=jnp.float32
    )


def to_sibling(value):
    return lax.ppermute(value, "core", [(0, 1), (1, 0)])


def at(stacked, index):
    return lax.dynamic_index_in_dim(stacked, index, 0, keepdims=False)


def ordered(own, other, core):
    return jnp.where(core == 0, jnp.stack([own, other]), jnp.stack([other, own]))


def ring_groups(along_y):
    groups = []
    for core in range(CORES):
        for z in range(Z):
            for other in range(4):
                places = [(other, k) if along_y[core] else (k, other) for k in range(4)]
                groups.append([((x * Z + z) * Y + y) * CORES + core for x, y in places])
    return groups


NEAR = ring_groups((True, False))
FAR = ring_groups((False, True))


def exchange(blocks, groups):
    return lax.all_to_all(blocks, AXES, 0, 0, axis_index_groups=groups, tiled=True)


def copies(value, count):
    return jnp.broadcast_to(value[None], (count,) + value.shape)


def add(*terms):
    total = terms[0].astype(jnp.float32)
    if len(terms) == 1:
        return jnp.sum(total, axis=0)
    for term in terms[1:]:
        total = total + term.astype(jnp.float32)
    return total


def step(value, axis, distance):
    return lax.ppermute(value, axis, [(i, (i + distance) % 4) for i in range(4)])


def gather_ring(own, axis):
    half = own.shape[0] // 2
    behind = step(own, axis, 1)
    ahead = step(own, axis, -1)
    far_low = step(behind[:half], axis, 1)
    far_high = step(ahead[half:], axis, -1)
    return jnp.stack([own, ahead, jnp.concatenate([far_low, far_high], axis=0), behind])


def scatter_ring(blocks, axis, between):
    half = blocks.shape[1] // 2

    def joined(own, received):
        return add(own, received).astype(own.dtype)

    low = step(blocks[2, :half], axis, 1)
    high = step(blocks[2, half:], axis, -1)
    low, high, between = lax.optimization_barrier((low, high, between))
    up = jnp.concatenate([joined(blocks[1, :half], low), blocks[1, half:]], axis=0)
    down = jnp.concatenate([blocks[3, :half], joined(blocks[3, half:], high)], axis=0)
    return add(blocks[0], step(up, axis, 1), step(down, axis, -1)), between


def rotated(blocks, shift):
    doubled = jnp.concatenate([blocks, blocks], axis=0)
    return lax.dynamic_slice_in_dim(doubled, shift, blocks.shape[0], 0)


def block_at(strides_ref, x, y, other=0):
    return x * strides_ref[2 * other] + y * strides_ref[2 * other + 1]


def blocks_spec(rows, features):
    return pl.BlockSpec((X * Y, 1, 2, rows, features), lambda i: (0, i, 0, 0, 0))


def project_kernel(strides_ref, encoder_ref, weight_ref, own_ref, sibling_ref, total_ref):
    index = pl.program_id(0)
    features = encoder_ref.shape[-1]
    encoder = jnp.concatenate(
        [
            jnp.concatenate(
                [
                    encoder_ref[block_at(strides_ref, x, y)].reshape(-1, features)
                    for x in range(X)
                ],
                axis=0,
            )
            for y in range(Y)
        ],
        axis=-1,
    )
    partial = product(encoder, weight_ref[0], COLS_BY_ROWS)

    @pl.when(index == 0)
    def _():
        total_ref[...] = partial

    @pl.when(index > 0)
    def _():
        total_ref[...] += partial

    @pl.when(index == Z // 2 - 1)
    def _():
        cols = own_ref.shape[-1]
        rounded = total_ref[...].astype(jnp.bfloat16)
        own_ref[...] = rounded[:, :cols].reshape(own_ref.shape)
        sibling_ref[...] = rounded[:, cols:].reshape(own_ref.shape)


def project(strides, encoder, weight):
    rows, features = encoder.shape[-2:]
    cols = weight.shape[-1]
    out = jax.ShapeDtypeStruct((X, 2 * rows, cols // 2), jnp.bfloat16)
    whole = pl.BlockSpec(out.shape, lambda i: (0, 0, 0))
    return pl.pallas_call(
        project_kernel,
        grid=(Z // 2,),
        out_shape=[out, out],
        in_specs=[
            IN_SMEM,
            blocks_spec(rows, features),
            pl.BlockSpec((1, Y * features, cols), lambda i: (i, 0, 0)),
        ],
        out_specs=[whole, whole],
        scratch_shapes=[pltpu.VMEM((X * 2 * rows, cols), jnp.float32)],
        compiler_params=pltpu.CompilerParams(vmem_limit_bytes=56 << 20),
        cost_estimate=pl.CostEstimate(
            flops=2_200_000_000, bytes_accessed=9_000_000, transcendentals=0
        ),
    )(strides, encoder, weight.reshape(Z // 2, Y * features, cols))


def term_kernel(strides_ref, own_ref, other_ref, weight_ref, out_ref):
    cols = own_ref.shape[-1]
    joined = jnp.concatenate(
        [ref[...].reshape(-1, cols) for ref in (own_ref, other_ref)], axis=-1
    )
    terms = product(joined, weight_ref[0], COLS_BY_COLS).astype(jnp.bfloat16)
    features = out_ref.shape[-1]
    size = terms.shape[0] // X
    for x in range(X):
        for y in range(Y):
            block = terms[x * size : (x + 1) * size, y * features : (y + 1) * features]
            out_ref[block_at(strides_ref, x, y)] = block.reshape(out_ref.shape[1:])


def encoder_terms(strides, own, other, weight):
    rows, cols = own.shape[1] // 2, weight.shape[-1]
    features = weight.shape[0] // GROUPS
    return pl.pallas_call(
        term_kernel,
        grid=(Z // 2,),
        out_shape=jax.ShapeDtypeStruct((X * Y, Z // 2, 2, rows, features), jnp.bfloat16),
        in_specs=[IN_SMEM]
        + [pl.BlockSpec(own.shape, lambda i: (0, 0, 0))] * 2
        + [pl.BlockSpec((1, Y * features, cols), lambda i: (i, 0, 0))],
        out_specs=blocks_spec(rows, features),
        compiler_params=pltpu.CompilerParams(vmem_limit_bytes=56 << 20),
        cost_estimate=pl.CostEstimate(
            flops=2_200_000_000, bytes_accessed=9_000_000, transcendentals=0
        ),
    )(strides, own, other, weight.reshape(Z // 2, Y * features, cols))


def weight_grad_kernel(
    strides_ref, encoder_ref, encoder_other_ref, own_ref, other_ref, key_ref, value_ref
):
    features = encoder_ref.shape[-1]
    cols = key_ref.shape[-1]
    grads = jnp.concatenate(
        [ref[...].reshape(-1, 2 * cols) for ref in (own_ref, other_ref)], axis=0
    )
    for y in range(Y):
        tokens = jnp.concatenate(
            [
                ref[block_at(strides_ref, x, y, other)].reshape(-1, features)
                for other, ref in enumerate((encoder_ref, encoder_other_ref))
                for x in range(X)
            ],
            axis=0,
        )
        both = product(tokens, grads, ROWS_BY_ROWS).astype(jnp.bfloat16)
        key_ref[y * features : (y + 1) * features] = both[:, :cols]
        value_ref[y * features : (y + 1) * features] = both[:, cols:]


def weight_grads(strides, encoder, encoder_other, own, other):
    rows, features = encoder.shape[-2:]
    cols = own.shape[-1] // 2
    out = jax.ShapeDtypeStruct((GROUPS * features, cols), jnp.bfloat16)
    return pl.pallas_call(
        weight_grad_kernel,
        grid=(Z // 2,),
        out_shape=[out, out],
        in_specs=[IN_SMEM]
        + [blocks_spec(rows, features)] * 2
        + [pl.BlockSpec(own.shape, lambda i: (0, 0, 0))] * 2,
        out_specs=[pl.BlockSpec((Y * features, cols), lambda i: (i, 0))] * 2,
        compiler_params=pltpu.CompilerParams(vmem_limit_bytes=56 << 20),
        cost_estimate=pl.CostEstimate(
            flops=2_200_000_000, bytes_accessed=11_000_000, transcendentals=0
        ),
    )(strides, encoder, encoder_other, own, other)


def attention_kernel(
    scale_ref,
    query_ref,
    grad_ref,
    own_ref,
    other_ref,
    attended_ref,
    grad_query_ref,
    grad_own_ref,
    grad_other_ref,
):
    rows = query_ref.shape[0] // SEQS
    cols = own_ref.shape[-1]
    places = X // SEQS
    for seq in range(SEQS):
        of_x = slice(seq * places, (seq + 1) * places)
        of_rows = slice(seq * rows, (seq + 1) * rows)
        kv = jnp.concatenate(
            [ref[of_x].reshape(-1, cols) for ref in (own_ref, other_ref)], axis=0
        )
        attended, grad_query, grad_key, grad_value = [], [], [], []
        for head in range(2):
            lanes = slice(head * HD, (head + 1) * HD)
            query, grad = query_ref[of_rows, lanes], grad_ref[of_rows, lanes]
            key, value = kv[:, : 2 * HD][:, lanes], kv[:, 2 * HD :][:, lanes]
            factor = scale_ref[0, head] * (1.0 / math.sqrt(HD))
            scores = product(query, key, COLS_BY_COLS) * factor
            powers = jnp.exp(scores - jnp.max(scores, axis=-1, keepdims=True))
            softmaxed = powers / jnp.sum(powers, axis=-1, keepdims=True)
            weights = softmaxed.astype(jnp.bfloat16)
            grad_weights = product(grad, value, COLS_BY_COLS)
            grad_scores = softmaxed * (
                grad_weights - jnp.sum(softmaxed * grad_weights, axis=-1, keepdims=True)
            )
            scaled = (grad_scores * factor).astype(jnp.bfloat16)
            attended.append(product(weights, value, COLS_BY_ROWS))
            grad_query.append(product(scaled, key, COLS_BY_ROWS))
            grad_key.append(product(scaled, query, ROWS_BY_ROWS))
            grad_value.append(product(weights, grad, ROWS_BY_ROWS))

        def joined(parts):
            return jnp.concatenate(parts, axis=-1).astype(jnp.bfloat16)

        attended_ref[of_rows] = joined(attended)
        grad_query_ref[of_rows] = joined(grad_query)
        grad_kv = joined(grad_key + grad_value)
        half = grad_kv.shape[0] // 2
        shape = (places,) + own_ref.shape[1:]
        grad_own_ref[of_x] = grad_kv[:half].reshape(shape)
        grad_other_ref[of_x] = grad_kv[half:].reshape(shape)


def attention(scale, query, grad, own, other):
    rows = jax.ShapeDtypeStruct(query.shape, query.dtype)
    tokens = jax.ShapeDtypeStruct(own.shape, own.dtype)
    return pl.pallas_call(
        attention_kernel,
        out_shape=[rows, rows, tokens, tokens],
        in_specs=[IN_SMEM] + [IN_VMEM] * 4,
        out_specs=[IN_VMEM] * 4,
        compiler_params=pltpu.CompilerParams(vmem_limit_bytes=24 << 20),
        cost_estimate=pl.CostEstimate(
            flops=210_000_000, bytes_accessed=1_500_000, transcendentals=270_000
        ),
    )(scale, query, grad, own, other)


def per_device(
    encoder_out,
    decoder_in,
    grad_output,
    query_weight,
    key_weight,
    value_weight,
    out_weight,
    head_scale,
):
    core, z_hi = lax.axis_index("core"), lax.axis_index("z_hi")
    far, near = 4 - 3 * core, 1 + 3 * core
    strides = jnp.stack([far, near, near, far]).astype(jnp.int32)
    local_query = query_weight[0]
    local_out = out_weight[0]
    tokens = encoder_out.shape[0]
    half, features = tokens // 2, 2 * tokens
    rows, width = decoder_in.shape[1:]
    cols = local_query.shape[1]
    dec_rows = Z // 2 * Y * CORES * rows

    floated = decoder_in[0].astype(jnp.float32)
    inv_rms = lax.rsqrt(jnp.mean(floated * floated, axis=-1, keepdims=True) + EPSILON)
    normed_full = floated * inv_rms
    normed = normed_full.astype(jnp.bfloat16)
    mine = jnp.where(core == 0, normed, grad_output[0])
    theirs = jnp.where(core == 0, grad_output[0], normed)
    block = ordered(mine, to_sibling(theirs), core).reshape(2 * rows, width)

    halves = encoder_out.reshape(2, half, tokens)
    piece = jnp.concatenate(
        list(ordered(at(halves, core), to_sibling(at(halves, 1 - core)), core)), axis=1
    )
    z_axes = ("z_hi", "z_lo")
    stack = lax.all_to_all(copies(piece, Z), z_axes, 0, 0, tiled=True)
    blocks = jnp.stack([block] + [step(block, "y", -k) for k in range(1, Y)])
    local_kv = [key_weight[0], value_weight[0]]
    joined_kv = jnp.concatenate(local_kv + [to_sibling(part) for part in local_kv], axis=1)
    stack, joined_kv, _ = lax.optimization_barrier((stack, joined_kv, blocks))
    encoder = exchange(copies(exchange(copies(stack, 4), NEAR), 4), FAR)
    encoder = encoder.reshape(X * Y, Z // 2, 2, half, features)
    gathered = gather_ring(blocks, "z_hi").reshape(dec_rows, width)

    query_halves = local_query.reshape(2, width // 2, cols)
    joined_query = jnp.concatenate(
        [at(query_halves, core), to_sibling(at(query_halves, 1 - core))], axis=1
    )
    out_columns = local_out.T
    row_weight = jnp.concatenate(
        [
            jnp.where(core == 0, local_query, out_columns),
            to_sibling(jnp.where(core == 0, out_columns, local_query)),
        ],
        axis=1,
    )

    made = jnp.dot(gathered, row_weight, preferred_element_type=jnp.float32).astype(jnp.bfloat16)
    by_place = (Z // 2, dec_rows // 4, -1)
    made = rotated(made.reshape(by_place), (4 - z_hi) % 4).reshape(dec_rows, -1)
    made_own, made_other = made[:, :cols], to_sibling(made[:, cols:])
    query_rows = jnp.where(core == 0, made_own, made_other)
    grad_attended = jnp.where(core == 0, made_other, made_own)
    kv_own, kv_sibling = project(strides, encoder, joined_kv)
    attended, grad_query, grad_kv_own, grad_kv_other = attention(
        head_scale, query_rows, grad_attended, kv_own, to_sibling(kv_sibling)
    )

    grad_kv_received = to_sibling(grad_kv_other)
    attended = rotated(attended.reshape(by_place), z_hi).reshape(dec_rows, cols)
    grad_query = rotated(grad_query.reshape(by_place), z_hi).reshape(dec_rows, cols)
    terms = encoder_terms(strides, grad_kv_own, grad_kv_received, joined_kv)
    query_joined = jnp.concatenate([grad_query, to_sibling(grad_query)], axis=1)
    terms, encoder, gathered, grad_query, query_joined = lax.optimization_barrier(
        (terms, encoder, gathered, grad_query, query_joined)
    )
    arrived = exchange(terms.reshape(4, 4, Z, half, features), FAR)

    others = to_sibling(gathered)
    normed_all = jnp.where(core == 0, gathered, others)
    cotangent = jnp.where(core == 0, others, gathered)
    out_weight_grad = product(attended, cotangent, ROWS_BY_ROWS).astype(jnp.bfloat16)
    query_weight_grad = product(normed_all, grad_query, ROWS_BY_ROWS).astype(jnp.bfloat16)
    key_weight_grad, value_weight_grad = weight_grads(
        strides, encoder, to_sibling(encoder), grad_kv_own, grad_kv_other
    )

    partial = product(query_joined, joined_query, COLS_BY_COLS).astype(jnp.bfloat16)
    partial = partial.reshape(Z // 2, Y, 2 * rows, width // 2)
    grads = (query_weight_grad, key_weight_grad, value_weight_grad, out_weight_grad)
    total, grads = scatter_ring(partial, "z_hi", grads)
    arrived, grads = lax.optimization_barrier((arrived, grads))
    query_weight_grad, key_weight_grad, value_weight_grad, out_weight_grad = grads
    total = total.astype(jnp.bfloat16)
    received = [step(total[k], "y", k) for k in range(1, Y)]
    arrived = exchange(add(arrived).astype(jnp.bfloat16), NEAR)
    arrived = lax.all_to_all(add(arrived).astype(jnp.bfloat16), z_axes, 0, 0, tiled=True)
    arrived, received = lax.optimization_barrier((arrived, received))
    total = add(total[0], *received)
    final = add(arrived)
    final = final.astype(jnp.bfloat16).reshape(half, 2, tokens).transpose(1, 0, 2)
    encoder_grad = ordered(
        at(final, core), to_sibling(at(final, 1 - core)), core
    ).reshape(tokens, tokens)

    total = total.reshape(2, rows, width // 2)
    grad_normed = jnp.concatenate(
        list(ordered(at(total, core), to_sibling(at(total, 1 - core)), core)), axis=1
    )
    decoder_grad = (
        (grad_normed - normed_full * jnp.mean(grad_normed * normed_full, axis=-1, keepdims=True))
        * inv_rms
    ).astype(jnp.bfloat16)

    return (
        encoder_grad,
        decoder_grad[None],
        query_weight_grad[None],
        key_weight_grad[None],
        value_weight_grad[None],
        out_weight_grad[None],
    )


def solution(mesh):
    section, tensor = AXES[:2], AXES[2:]
    placed = (
        P(section, tensor),
        P(section, tensor, None),
        P(section, tensor, None),
        P(section, None, tensor),
        P(section, None, tensor),
        P(section, None, tensor),
        P(section, tensor, None),
        P(section, tensor),
    )
    return jax.shard_map(
        per_device,
        mesh=Mesh(mesh.devices.reshape(X, 2, Z // 2, Y, CORES), AXES),
        in_specs=placed,
        out_specs=placed[:2] + placed[3:7],
        check_vma=False,
    )
```

```python
import math

import jax
import jax.numpy as jnp
from jax import lax
from jax.experimental import pallas as pl
from jax.experimental.pallas import tpu as pltpu
from jax.sharding import Mesh, PartitionSpec as P

HD = 64
SEQS = 2
EPSILON = 1e-06
AXES = ("x", "z_lo", "z_hi", "y", "core")
X, Z, Y, CORES = 4, 8, 4, 2
GROUPS = 16
ROWS_BY_ROWS = (((0,), (0,)), ((), ()))
COLS_BY_COLS = (((1,), (1,)), ((), ()))
COLS_BY_ROWS = (((1,), (0,)), ((), ()))
IN_SMEM = pl.BlockSpec(memory_space=pltpu.SMEM)
IN_VMEM = pl.BlockSpec(memory_space=pltpu.VMEM)


def product(first_matrix, second_matrix, contracted):
    return lax.dot_general(
        first_matrix, second_matrix, contracted, preferred_element_type=jnp.float32
    )


def to_sibling(value):
    return lax.ppermute(value, "core", [(0, 1), (1, 0)])


def at(stacked, index):
    return lax.dynamic_index_in_dim(stacked, index, 0, keepdims=False)


def ordered(own, other, core):
    return jnp.where(core == 0, jnp.stack([own, other]), jnp.stack([other, own]))


def ring_groups(along_y):
    groups = []
    for core in range(CORES):
        for z in range(Z):
            for other in range(4):
                places = [(other, k) if along_y[core] else (k, other) for k in range(4)]
                groups.append([((x * Z + z) * Y + y) * CORES + core for x, y in places])
    return groups


NEAR = ring_groups((True, False))
FAR = ring_groups((False, True))


def exchange(blocks, groups):
    return lax.all_to_all(blocks, AXES, 0, 0, axis_index_groups=groups, tiled=True)


def copies(value, count):
    return jnp.broadcast_to(value[None], (count,) + value.shape)


def add(*terms):
    total = terms[0].astype(jnp.float32)
    if len(terms) == 1:
        return jnp.sum(total, axis=0)
    for term in terms[1:]:
        total = total + term.astype(jnp.float32)
    return total


FIRST, LAST = (False, True), (True, False)


def step(value, along_y, distance):
    pairs = []
    for device in range(X * Z * Y * CORES):
        core, y, z_hi = device % 2, device // 2 % 4, device // 8 % 4
        if along_y[core]:
            target = device + ((y + distance) % 4 - y) * 2
        else:
            target = device + ((z_hi + distance) % 4 - z_hi) * 8
        pairs.append((device, target))
    return lax.ppermute(value, AXES, pairs)


def first_steps(own, along_y):
    return step(own, along_y, 1), step(own, along_y, -1)


def last_steps(own, behind, ahead, along_y):
    half = own.shape[0] // 2
    far_low = step(behind[:half], along_y, 1)
    far_high = step(ahead[half:], along_y, -1)
    return jnp.stack([own, ahead, jnp.concatenate([far_low, far_high], axis=0), behind])


def scatter_ring(blocks, along_y, between):
    half = blocks.shape[1] // 2

    def joined(own, received):
        return add(own, received).astype(own.dtype)

    low = step(blocks[2, :half], along_y, 1)
    high = step(blocks[2, half:], along_y, -1)
    low, high, between = lax.optimization_barrier((low, high, between))
    up = jnp.concatenate([joined(blocks[1, :half], low), blocks[1, half:]], axis=0)
    down = jnp.concatenate([blocks[3, :half], joined(blocks[3, half:], high)], axis=0)
    return add(blocks[0], step(up, along_y, 1), step(down, along_y, -1)), between


def rotated(blocks, shift):
    doubled = jnp.concatenate([blocks, blocks], axis=0)
    return lax.dynamic_slice_in_dim(doubled, shift, blocks.shape[0], 0)


def block_at(strides_ref, x, y, other=0):
    return x * strides_ref[2 * other] + y * strides_ref[2 * other + 1]


def blocks_spec(rows, features):
    return pl.BlockSpec((X * Y, 1, 2, rows, features), lambda i: (0, i, 0, 0, 0))


def project_kernel(strides_ref, encoder_ref, weight_ref, own_ref, sibling_ref, total_ref):
    index = pl.program_id(0)
    features = encoder_ref.shape[-1]
    encoder = jnp.concatenate(
        [
            jnp.concatenate(
                [
                    encoder_ref[block_at(strides_ref, x, y)].reshape(-1, features)
                    for x in range(X)
                ],
                axis=0,
            )
            for y in range(Y)
        ],
        axis=-1,
    )
    partial = product(encoder, weight_ref[0], COLS_BY_ROWS)

    @pl.when(index == 0)
    def _():
        total_ref[...] = partial

    @pl.when(index > 0)
    def _():
        total_ref[...] += partial

    @pl.when(index == Z // 2 - 1)
    def _():
        cols = own_ref.shape[-1]
        rounded = total_ref[...].astype(jnp.bfloat16)
        own_ref[...] = rounded[:, :cols].reshape(own_ref.shape)
        sibling_ref[...] = rounded[:, cols:].reshape(own_ref.shape)


def project(strides, encoder, weight):
    rows, features = encoder.shape[-2:]
    cols = weight.shape[-1]
    out = jax.ShapeDtypeStruct((X, 2 * rows, cols // 2), jnp.bfloat16)
    whole = pl.BlockSpec(out.shape, lambda i: (0, 0, 0))
    return pl.pallas_call(
        project_kernel,
        grid=(Z // 2,),
        out_shape=[out, out],
        in_specs=[
            IN_SMEM,
            blocks_spec(rows, features),
            pl.BlockSpec((1, Y * features, cols), lambda i: (i, 0, 0)),
        ],
        out_specs=[whole, whole],
        scratch_shapes=[pltpu.VMEM((X * 2 * rows, cols), jnp.float32)],
        compiler_params=pltpu.CompilerParams(vmem_limit_bytes=56 << 20),
        cost_estimate=pl.CostEstimate(
            flops=2_200_000_000, bytes_accessed=9_000_000, transcendentals=0
        ),
    )(strides, encoder, weight.reshape(Z // 2, Y * features, cols))


def term_kernel(strides_ref, own_ref, other_ref, weight_ref, out_ref):
    cols = own_ref.shape[-1]
    joined = jnp.concatenate(
        [ref[...].reshape(-1, cols) for ref in (own_ref, other_ref)], axis=-1
    )
    terms = product(joined, weight_ref[0], COLS_BY_COLS).astype(jnp.bfloat16)
    features = out_ref.shape[-1]
    size = terms.shape[0] // X
    for x in range(X):
        for y in range(Y):
            block = terms[x * size : (x + 1) * size, y * features : (y + 1) * features]
            out_ref[block_at(strides_ref, x, y)] = block.reshape(out_ref.shape[1:])


def encoder_terms(strides, own, other, weight):
    rows, cols = own.shape[1] // 2, weight.shape[-1]
    features = weight.shape[0] // GROUPS
    return pl.pallas_call(
        term_kernel,
        grid=(Z // 2,),
        out_shape=jax.ShapeDtypeStruct((X * Y, Z // 2, 2, rows, features), jnp.bfloat16),
        in_specs=[IN_SMEM]
        + [pl.BlockSpec(own.shape, lambda i: (0, 0, 0))] * 2
        + [pl.BlockSpec((1, Y * features, cols), lambda i: (i, 0, 0))],
        out_specs=blocks_spec(rows, features),
        compiler_params=pltpu.CompilerParams(vmem_limit_bytes=56 << 20),
        cost_estimate=pl.CostEstimate(
            flops=2_200_000_000, bytes_accessed=9_000_000, transcendentals=0
        ),
    )(strides, own, other, weight.reshape(Z // 2, Y * features, cols))


def weight_grad_kernel(
    strides_ref, encoder_ref, encoder_other_ref, own_ref, other_ref, key_ref, value_ref
):
    features = encoder_ref.shape[-1]
    cols = key_ref.shape[-1]
    grads = jnp.concatenate(
        [ref[...].reshape(-1, 2 * cols) for ref in (own_ref, other_ref)], axis=0
    )
    for y in range(Y):
        tokens = jnp.concatenate(
            [
                ref[block_at(strides_ref, x, y, other)].reshape(-1, features)
                for other, ref in enumerate((encoder_ref, encoder_other_ref))
                for x in range(X)
            ],
            axis=0,
        )
        both = product(tokens, grads, ROWS_BY_ROWS).astype(jnp.bfloat16)
        key_ref[y * features : (y + 1) * features] = both[:, :cols]
        value_ref[y * features : (y + 1) * features] = both[:, cols:]


def weight_grads(strides, encoder, encoder_other, own, other):
    rows, features = encoder.shape[-2:]
    cols = own.shape[-1] // 2
    out = jax.ShapeDtypeStruct((GROUPS * features, cols), jnp.bfloat16)
    return pl.pallas_call(
        weight_grad_kernel,
        grid=(Z // 2,),
        out_shape=[out, out],
        in_specs=[IN_SMEM]
        + [blocks_spec(rows, features)] * 2
        + [pl.BlockSpec(own.shape, lambda i: (0, 0, 0))] * 2,
        out_specs=[pl.BlockSpec((Y * features, cols), lambda i: (i, 0))] * 2,
        compiler_params=pltpu.CompilerParams(vmem_limit_bytes=56 << 20),
        cost_estimate=pl.CostEstimate(
            flops=2_200_000_000, bytes_accessed=11_000_000, transcendentals=0
        ),
    )(strides, encoder, encoder_other, own, other)


def attention_kernel(
    scale_ref,
    query_ref,
    grad_ref,
    own_ref,
    other_ref,
    attended_ref,
    grad_query_ref,
    grad_own_ref,
    grad_other_ref,
):
    rows = query_ref.shape[0] // SEQS
    cols = own_ref.shape[-1]
    places = X // SEQS
    for seq in range(SEQS):
        of_x = slice(seq * places, (seq + 1) * places)
        of_rows = slice(seq * rows, (seq + 1) * rows)
        kv = jnp.concatenate(
            [ref[of_x].reshape(-1, cols) for ref in (own_ref, other_ref)], axis=0
        )
        attended, grad_query, grad_key, grad_value = [], [], [], []
        for head in range(2):
            lanes = slice(head * HD, (head + 1) * HD)
            query, grad = query_ref[of_rows, lanes], grad_ref[of_rows, lanes]
            key, value = kv[:, : 2 * HD][:, lanes], kv[:, 2 * HD :][:, lanes]
            factor = scale_ref[0, head] * (1.0 / math.sqrt(HD))
            scores = product(query, key, COLS_BY_COLS) * factor
            powers = jnp.exp(scores - jnp.max(scores, axis=-1, keepdims=True))
            softmaxed = powers / jnp.sum(powers, axis=-1, keepdims=True)
            weights = softmaxed.astype(jnp.bfloat16)
            grad_weights = product(grad, value, COLS_BY_COLS)
            grad_scores = softmaxed * (
                grad_weights - jnp.sum(softmaxed * grad_weights, axis=-1, keepdims=True)
            )
            scaled = (grad_scores * factor).astype(jnp.bfloat16)
            attended.append(product(weights, value, COLS_BY_ROWS))
            grad_query.append(product(scaled, key, COLS_BY_ROWS))
            grad_key.append(product(scaled, query, ROWS_BY_ROWS))
            grad_value.append(product(weights, grad, ROWS_BY_ROWS))

        def joined(parts):
            return jnp.concatenate(parts, axis=-1).astype(jnp.bfloat16)

        attended_ref[of_rows] = joined(attended)
        grad_query_ref[of_rows] = joined(grad_query)
        grad_kv = joined(grad_key + grad_value)
        half = grad_kv.shape[0] // 2
        shape = (places,) + own_ref.shape[1:]
        grad_own_ref[of_x] = grad_kv[:half].reshape(shape)
        grad_other_ref[of_x] = grad_kv[half:].reshape(shape)


def attention(scale, query, grad, own, other):
    rows = jax.ShapeDtypeStruct(query.shape, query.dtype)
    tokens = jax.ShapeDtypeStruct(own.shape, own.dtype)
    return pl.pallas_call(
        attention_kernel,
        out_shape=[rows, rows, tokens, tokens],
        in_specs=[IN_SMEM] + [IN_VMEM] * 4,
        out_specs=[IN_VMEM] * 4,
        compiler_params=pltpu.CompilerParams(vmem_limit_bytes=24 << 20),
        cost_estimate=pl.CostEstimate(
            flops=210_000_000, bytes_accessed=1_500_000, transcendentals=270_000
        ),
    )(scale, query, grad, own, other)


def per_device(
    encoder_out,
    decoder_in,
    grad_output,
    query_weight,
    key_weight,
    value_weight,
    out_weight,
    head_scale,
):
    core, z_hi = lax.axis_index("core"), lax.axis_index("z_hi")
    far, near = 4 - 3 * core, 1 + 3 * core
    strides = jnp.stack([far, near, near, far]).astype(jnp.int32)
    local_query = query_weight[0]
    local_out = out_weight[0]
    tokens = encoder_out.shape[0]
    half, features = tokens // 2, 2 * tokens
    rows, width = decoder_in.shape[1:]
    cols = local_query.shape[1]
    dec_rows = Z // 2 * Y * CORES * rows

    floated = decoder_in[0].astype(jnp.float32)
    inv_rms = lax.rsqrt(jnp.mean(floated * floated, axis=-1, keepdims=True) + EPSILON)
    normed_full = floated * inv_rms
    normed = normed_full.astype(jnp.bfloat16)
    mine = jnp.where(core == 0, normed, grad_output[0])
    theirs = jnp.where(core == 0, grad_output[0], normed)
    block = ordered(mine, to_sibling(theirs), core).reshape(2 * rows, width)

    halves = encoder_out.reshape(2, half, tokens)
    piece = jnp.concatenate(
        list(ordered(at(halves, core), to_sibling(at(halves, 1 - core)), core)), axis=1
    )
    z_axes = ("z_hi", "z_lo")
    stack = lax.all_to_all(copies(piece, Z), z_axes, 0, 0, tiled=True)
    blocks = jnp.stack([block] + [step(block, FIRST, -k) for k in range(1, Y)])
    local_kv = [key_weight[0], value_weight[0]]
    joined_kv = jnp.concatenate(local_kv + [to_sibling(part) for part in local_kv], axis=1)
    stack, joined_kv, _ = lax.optimization_barrier((stack, joined_kv, blocks))
    behind, ahead = first_steps(blocks, LAST)
    encoder = exchange(copies(stack, 4), NEAR)
    encoder, behind, ahead = lax.optimization_barrier((encoder, behind, ahead))
    encoder = exchange(copies(encoder, 4), FAR).reshape(X * Y, Z // 2, 2, half, features)
    gathered = last_steps(blocks, behind, ahead, LAST).reshape(dec_rows, width)

    query_halves = local_query.reshape(2, width // 2, cols)
    joined_query = jnp.concatenate(
        [at(query_halves, core), to_sibling(at(query_halves, 1 - core))], axis=1
    )
    out_columns = local_out.T
    row_weight = jnp.concatenate(
        [
            jnp.where(core == 0, local_query, out_columns),
            to_sibling(jnp.where(core == 0, out_columns, local_query)),
        ],
        axis=1,
    )

    made = jnp.dot(gathered, row_weight, preferred_element_type=jnp.float32).astype(jnp.bfloat16)
    made_own, made_other = made[:, :cols], to_sibling(made[:, cols:])
    query_rows = jnp.where(core == 0, made_own, made_other)
    grad_attended = jnp.where(core == 0, made_other, made_own)
    by_place = (4, 4, 2 * rows, -1)

    def swapped(values):
        shape = values.shape
        return values.reshape(by_place).transpose(1, 0, 2, 3).reshape(shape)

    def turned(values, shift):
        return rotated(values.reshape(by_place), shift).reshape(values.shape)

    query_rows = turned(swapped(query_rows), (4 - z_hi) % 4)
    grad_attended = turned(grad_attended, (4 - z_hi) % 4)
    kv_own, kv_sibling = project(strides, encoder, joined_kv)
    attended, grad_query, grad_kv_own, grad_kv_other = attention(
        head_scale, query_rows, grad_attended, kv_own, to_sibling(kv_sibling)
    )

    grad_kv_received = to_sibling(grad_kv_other)
    attended, grad_query = turned(attended, z_hi), swapped(turned(grad_query, z_hi))
    terms = encoder_terms(strides, grad_kv_own, grad_kv_received, joined_kv)
    query_joined = jnp.concatenate([grad_query, to_sibling(grad_query)], axis=1)
    query_joined = jnp.where(core == 0, query_joined, swapped(query_joined))
    terms, encoder, gathered, grad_query, query_joined = lax.optimization_barrier(
        (terms, encoder, gathered, grad_query, query_joined)
    )
    arrived = exchange(terms.reshape(4, 4, Z, half, features), FAR)

    others = to_sibling(gathered)
    normed_all = jnp.where(core == 0, gathered, others)
    cotangent = jnp.where(core == 0, others, gathered)
    out_weight_grad = product(attended, cotangent, ROWS_BY_ROWS).astype(jnp.bfloat16)
    query_weight_grad = product(normed_all, grad_query, ROWS_BY_ROWS).astype(jnp.bfloat16)
    key_weight_grad, value_weight_grad = weight_grads(
        strides, encoder, to_sibling(encoder), grad_kv_own, grad_kv_other
    )

    partial = product(query_joined, joined_query, COLS_BY_COLS).astype(jnp.bfloat16)
    partial = partial.reshape(Z // 2, Y, 2 * rows, width // 2)
    grads = (query_weight_grad, key_weight_grad, value_weight_grad, out_weight_grad)
    total, grads = scatter_ring(partial, LAST, grads)
    arrived, grads = lax.optimization_barrier((arrived, grads))
    query_weight_grad, key_weight_grad, value_weight_grad, out_weight_grad = grads
    total = total.astype(jnp.bfloat16)
    received = [step(total[k], FIRST, k) for k in range(1, Y)]
    arrived = exchange(add(arrived).astype(jnp.bfloat16), NEAR)
    arrived = lax.all_to_all(add(arrived).astype(jnp.bfloat16), z_axes, 0, 0, tiled=True)
    arrived, received = lax.optimization_barrier((arrived, received))
    total = add(total[0], *received)
    final = add(arrived)
    final = final.astype(jnp.bfloat16).reshape(half, 2, tokens).transpose(1, 0, 2)
    encoder_grad = ordered(
        at(final, core), to_sibling(at(final, 1 - core)), core
    ).reshape(tokens, tokens)

    total = total.reshape(2, rows, width // 2)
    grad_normed = jnp.concatenate(
        list(ordered(at(total, core), to_sibling(at(total, 1 - core)), core)), axis=1
    )
    decoder_grad = (
        (grad_normed - normed_full * jnp.mean(grad_normed * normed_full, axis=-1, keepdims=True))
        * inv_rms
    ).astype(jnp.bfloat16)

    return (
        encoder_grad,
        decoder_grad[None],
        query_weight_grad[None],
        key_weight_grad[None],
        value_weight_grad[None],
        out_weight_grad[None],
    )


def solution(mesh):
    section, tensor = AXES[:2], AXES[2:]
    placed = (
        P(section, tensor),
        P(section, tensor, None),
        P(section, tensor, None),
        P(section, None, tensor),
        P(section, None, tensor),
        P(section, None, tensor),
        P(section, tensor, None),
        P(section, tensor),
    )
    return jax.shard_map(
        per_device,
        mesh=Mesh(mesh.devices.reshape(X, 2, Z // 2, Y, CORES), AXES),
        in_specs=placed,
        out_specs=placed[:2] + placed[3:7],
        check_vma=False,
    )
```

```python
import math

import jax
import jax.numpy as jnp
from jax import lax
from jax.experimental import pallas as pl
from jax.experimental.pallas import tpu as pltpu
from jax.sharding import Mesh, PartitionSpec as P

HD = 64
SEQS = 2
EPSILON = 1e-06
AXES = ("x", "z_lo", "z_hi", "y", "core")
X, Z, Y, CORES = 4, 8, 4, 2
GROUPS = 16
ROWS_BY_ROWS = (((0,), (0,)), ((), ()))
COLS_BY_COLS = (((1,), (1,)), ((), ()))
COLS_BY_ROWS = (((1,), (0,)), ((), ()))
IN_SMEM = pl.BlockSpec(memory_space=pltpu.SMEM)
IN_VMEM = pl.BlockSpec(memory_space=pltpu.VMEM)


def product(first_matrix, second_matrix, contracted):
    return lax.dot_general(
        first_matrix, second_matrix, contracted, preferred_element_type=jnp.float32
    )


def to_sibling(value):
    return lax.ppermute(value, "core", [(0, 1), (1, 0)])


def at(stacked, index):
    return lax.dynamic_index_in_dim(stacked, index, 0, keepdims=False)


def ordered(own, other, core):
    return jnp.where(core == 0, jnp.stack([own, other]), jnp.stack([other, own]))


def ring_groups(along_y):
    groups = []
    for core in range(CORES):
        for z in range(Z):
            for other in range(4):
                places = [(other, k) if along_y[core] else (k, other) for k in range(4)]
                groups.append([((x * Z + z) * Y + y) * CORES + core for x, y in places])
    return groups


NEAR = ring_groups((True, False))
FAR = ring_groups((False, True))


def exchange(blocks, groups):
    return lax.all_to_all(blocks, AXES, 0, 0, axis_index_groups=groups, tiled=True)


def copies(value, count):
    return jnp.broadcast_to(value[None], (count,) + value.shape)


def spread_kernel(value_ref, out_ref, sems):
    sends = [
        pltpu.make_async_copy(value_ref, out_ref.at[k], sems.at[k])
        for k in range(out_ref.shape[0])
    ]
    for send in sends:
        send.start()
    for send in sends:
        send.wait()


def spread(value, count):
    shape = (count,) + value.shape
    return pl.pallas_call(
        spread_kernel,
        out_shape=jax.ShapeDtypeStruct(shape, value.dtype),
        in_specs=[IN_VMEM],
        out_specs=pl.BlockSpec(memory_space=pl.ANY),
        scratch_shapes=[pltpu.SemaphoreType.DMA((count,))],
        compiler_params=pltpu.CompilerParams(vmem_limit_bytes=8 << 20),
        cost_estimate=pl.CostEstimate(flops=0, bytes_accessed=5_000_000, transcendentals=0),
    )(value)


def add(*terms):
    total = terms[0].astype(jnp.float32)
    if len(terms) == 1:
        return jnp.sum(total, axis=0)
    for term in terms[1:]:
        total = total + term.astype(jnp.float32)
    return total


FIRST, LAST = (False, True), (True, False)


def step(value, along_y, distance):
    pairs = []
    for device in range(X * Z * Y * CORES):
        core, y, z_hi = device % 2, device // 2 % 4, device // 8 % 4
        if along_y[core]:
            target = device + ((y + distance) % 4 - y) * 2
        else:
            target = device + ((z_hi + distance) % 4 - z_hi) * 8
        pairs.append((device, target))
    return lax.ppermute(value, AXES, pairs)


def first_steps(own, along_y):
    return step(own, along_y, 1), step(own, along_y, -1)


def last_steps(own, behind, ahead, along_y):
    half = own.shape[0] // 2
    far_low = step(behind[:half], along_y, 1)
    far_high = step(ahead[half:], along_y, -1)
    return jnp.stack([own, ahead, jnp.concatenate([far_low, far_high], axis=0), behind])


def scatter_ring(blocks, along_y, between):
    half = blocks.shape[1] // 2

    def joined(own, received):
        return add(own, received).astype(own.dtype)

    low = step(blocks[2, :half], along_y, 1)
    high = step(blocks[2, half:], along_y, -1)
    low, high, between = lax.optimization_barrier((low, high, between))
    up = jnp.concatenate([joined(blocks[1, :half], low), blocks[1, half:]], axis=0)
    down = jnp.concatenate([blocks[3, :half], joined(blocks[3, half:], high)], axis=0)
    return add(blocks[0], step(up, along_y, 1), step(down, along_y, -1)), between


def rotated(blocks, shift):
    doubled = jnp.concatenate([blocks, blocks], axis=0)
    return lax.dynamic_slice_in_dim(doubled, shift, blocks.shape[0], 0)


def block_at(strides_ref, x, y, other=0):
    return x * strides_ref[2 * other] + y * strides_ref[2 * other + 1]


def blocks_spec(rows, features):
    return pl.BlockSpec((X * Y, 1, 2, rows, features), lambda i: (0, i, 0, 0, 0))


def project_kernel(
    strides_ref, encoder_hbm, weight_hbm, own_ref, sibling_ref, encoder_ref, weight_ref, sems
):
    loads = []
    for index in range(Z // 2):
        loads.append(
            (
                pltpu.make_async_copy(
                    encoder_hbm.at[:, index], encoder_ref.at[index], sems.at[0, index]
                ),
                pltpu.make_async_copy(
                    weight_hbm.at[index], weight_ref.at[index], sems.at[1, index]
                ),
            )
        )
        for load in loads[-1]:
            load.start()
    features = encoder_ref.shape[-1]
    total = None
    for index in range(Z // 2):
        for load in loads[index]:
            load.wait()
        encoder = jnp.concatenate(
            [
                jnp.concatenate(
                    [
                        encoder_ref[index, block_at(strides_ref, x, y)].reshape(-1, features)
                        for x in range(X)
                    ],
                    axis=0,
                )
                for y in range(Y)
            ],
            axis=-1,
        )
        partial = product(encoder, weight_ref[index], COLS_BY_ROWS)
        total = partial if total is None else total + partial
    cols = own_ref.shape[-1]
    rounded = total.astype(jnp.bfloat16)
    own_ref[...] = rounded[:, :cols].reshape(own_ref.shape)
    sibling_ref[...] = rounded[:, cols:].reshape(own_ref.shape)


def project(strides, encoder, weight):
    rows, features = encoder.shape[-2:]
    cols = weight.shape[-1]
    out = jax.ShapeDtypeStruct((X, 2 * rows, cols // 2), jnp.bfloat16)
    weight = weight.reshape(Z // 2, Y * features, cols)
    return pl.pallas_call(
        project_kernel,
        out_shape=[out, out],
        in_specs=[IN_SMEM] + [pl.BlockSpec(memory_space=pl.ANY)] * 2,
        out_specs=[IN_VMEM] * 2,
        scratch_shapes=[
            pltpu.VMEM((Z // 2, X * Y, 2, rows, features), jnp.bfloat16),
            pltpu.VMEM(weight.shape, jnp.bfloat16),
            pltpu.SemaphoreType.DMA((2, Z // 2)),
        ],
        compiler_params=pltpu.CompilerParams(vmem_limit_bytes=56 << 20),
        cost_estimate=pl.CostEstimate(
            flops=2_200_000_000, bytes_accessed=9_000_000, transcendentals=0
        ),
    )(strides, encoder, weight)


def term_kernel(strides_ref, own_ref, other_ref, weight_ref, out_ref):
    cols = own_ref.shape[-1]
    joined = jnp.concatenate(
        [ref[...].reshape(-1, cols) for ref in (own_ref, other_ref)], axis=-1
    )
    terms = product(joined, weight_ref[0], COLS_BY_COLS).astype(jnp.bfloat16)
    features = out_ref.shape[-1]
    size = terms.shape[0] // X
    for x in range(X):
        for y in range(Y):
            block = terms[x * size : (x + 1) * size, y * features : (y + 1) * features]
            out_ref[block_at(strides_ref, x, y)] = block.reshape(out_ref.shape[1:])


def encoder_terms(strides, own, other, weight):
    rows, cols = own.shape[1] // 2, weight.shape[-1]
    features = weight.shape[0] // GROUPS
    return pl.pallas_call(
        term_kernel,
        grid=(Z // 2,),
        out_shape=jax.ShapeDtypeStruct((X * Y, Z // 2, 2, rows, features), jnp.bfloat16),
        in_specs=[IN_SMEM]
        + [pl.BlockSpec(own.shape, lambda i: (0, 0, 0))] * 2
        + [pl.BlockSpec((1, Y * features, cols), lambda i: (i, 0, 0))],
        out_specs=blocks_spec(rows, features),
        compiler_params=pltpu.CompilerParams(vmem_limit_bytes=56 << 20),
        cost_estimate=pl.CostEstimate(
            flops=2_200_000_000, bytes_accessed=9_000_000, transcendentals=0
        ),
    )(strides, own, other, weight.reshape(Z // 2, Y * features, cols))


def weight_grad_kernel(
    strides_ref, encoder_ref, encoder_other_ref, own_ref, other_ref, key_ref, value_ref
):
    features = encoder_ref.shape[-1]
    cols = key_ref.shape[-1]
    grads = jnp.concatenate(
        [ref[...].reshape(-1, 2 * cols) for ref in (own_ref, other_ref)], axis=0
    )
    for y in range(Y):
        tokens = jnp.concatenate(
            [
                ref[block_at(strides_ref, x, y, other)].reshape(-1, features)
                for other, ref in enumerate((encoder_ref, encoder_other_ref))
                for x in range(X)
            ],
            axis=0,
        )
        both = product(tokens, grads, ROWS_BY_ROWS).astype(jnp.bfloat16)
        key_ref[y * features : (y + 1) * features] = both[:, :cols]
        value_ref[y * features : (y + 1) * features] = both[:, cols:]


def weight_grads(strides, encoder, encoder_other, own, other):
    rows, features = encoder.shape[-2:]
    cols = own.shape[-1] // 2
    out = jax.ShapeDtypeStruct((GROUPS * features, cols), jnp.bfloat16)
    return pl.pallas_call(
        weight_grad_kernel,
        grid=(Z // 2,),
        out_shape=[out, out],
        in_specs=[IN_SMEM]
        + [blocks_spec(rows, features)] * 2
        + [pl.BlockSpec(own.shape, lambda i: (0, 0, 0))] * 2,
        out_specs=[pl.BlockSpec((Y * features, cols), lambda i: (i, 0))] * 2,
        compiler_params=pltpu.CompilerParams(vmem_limit_bytes=56 << 20),
        cost_estimate=pl.CostEstimate(
            flops=2_200_000_000, bytes_accessed=11_000_000, transcendentals=0
        ),
    )(strides, encoder, encoder_other, own, other)


def attention_kernel(
    scale_ref,
    query_ref,
    grad_ref,
    own_ref,
    other_ref,
    attended_ref,
    grad_query_ref,
    grad_own_ref,
    grad_other_ref,
):
    rows = query_ref.shape[0] // SEQS
    cols = own_ref.shape[-1]
    places = X // SEQS
    for seq in range(SEQS):
        of_x = slice(seq * places, (seq + 1) * places)
        of_rows = slice(seq * rows, (seq + 1) * rows)
        kv = jnp.concatenate(
            [ref[of_x].reshape(-1, cols) for ref in (own_ref, other_ref)], axis=0
        )
        attended, grad_query, grad_key, grad_value = [], [], [], []
        for head in range(2):
            lanes = slice(head * HD, (head + 1) * HD)
            query, grad = query_ref[of_rows, lanes], grad_ref[of_rows, lanes]
            key, value = kv[:, : 2 * HD][:, lanes], kv[:, 2 * HD :][:, lanes]
            factor = scale_ref[0, head] * (1.0 / math.sqrt(HD))
            scores = product(query, key, COLS_BY_COLS) * factor
            powers = jnp.exp(scores - jnp.max(scores, axis=-1, keepdims=True))
            softmaxed = powers / jnp.sum(powers, axis=-1, keepdims=True)
            weights = softmaxed.astype(jnp.bfloat16)
            grad_weights = product(grad, value, COLS_BY_COLS)
            grad_scores = softmaxed * (
                grad_weights - jnp.sum(softmaxed * grad_weights, axis=-1, keepdims=True)
            )
            scaled = (grad_scores * factor).astype(jnp.bfloat16)
            attended.append(product(weights, value, COLS_BY_ROWS))
            grad_query.append(product(scaled, key, COLS_BY_ROWS))
            grad_key.append(product(scaled, query, ROWS_BY_ROWS))
            grad_value.append(product(weights, grad, ROWS_BY_ROWS))

        def joined(parts):
            return jnp.concatenate(parts, axis=-1).astype(jnp.bfloat16)

        attended_ref[of_rows] = joined(attended)
        grad_query_ref[of_rows] = joined(grad_query)
        grad_kv = joined(grad_key + grad_value)
        half = grad_kv.shape[0] // 2
        shape = (places,) + own_ref.shape[1:]
        grad_own_ref[of_x] = grad_kv[:half].reshape(shape)
        grad_other_ref[of_x] = grad_kv[half:].reshape(shape)


def attention(scale, query, grad, own, other):
    rows = jax.ShapeDtypeStruct(query.shape, query.dtype)
    tokens = jax.ShapeDtypeStruct(own.shape, own.dtype)
    return pl.pallas_call(
        attention_kernel,
        out_shape=[rows, rows, tokens, tokens],
        in_specs=[IN_SMEM] + [IN_VMEM] * 4,
        out_specs=[IN_VMEM] * 4,
        compiler_params=pltpu.CompilerParams(vmem_limit_bytes=24 << 20),
        cost_estimate=pl.CostEstimate(
            flops=210_000_000, bytes_accessed=1_500_000, transcendentals=270_000
        ),
    )(scale, query, grad, own, other)


def per_device(
    encoder_out,
    decoder_in,
    grad_output,
    query_weight,
    key_weight,
    value_weight,
    out_weight,
    head_scale,
):
    core, z_hi = lax.axis_index("core"), lax.axis_index("z_hi")
    far, near = 4 - 3 * core, 1 + 3 * core
    strides = jnp.stack([far, near, near, far]).astype(jnp.int32)
    local_query = query_weight[0]
    local_out = out_weight[0]
    tokens = encoder_out.shape[0]
    half, features = tokens // 2, 2 * tokens
    rows, width = decoder_in.shape[1:]
    cols = local_query.shape[1]
    dec_rows = Z // 2 * Y * CORES * rows

    floated = decoder_in[0].astype(jnp.float32)
    inv_rms = lax.rsqrt(jnp.mean(floated * floated, axis=-1, keepdims=True) + EPSILON)
    normed_full = floated * inv_rms
    normed = normed_full.astype(jnp.bfloat16)
    mine = jnp.where(core == 0, normed, grad_output[0])
    theirs = jnp.where(core == 0, grad_output[0], normed)
    block = ordered(mine, to_sibling(theirs), core).reshape(2 * rows, width)

    halves = encoder_out.reshape(2, half, tokens)
    piece = jnp.concatenate(
        list(ordered(at(halves, core), to_sibling(at(halves, 1 - core)), core)), axis=1
    )
    z_axes = ("z_hi", "z_lo")
    stack = lax.all_to_all(copies(piece, Z), z_axes, 0, 0, tiled=True)
    blocks = jnp.stack([block] + [step(block, FIRST, -k) for k in range(1, Y)])
    local_kv = [key_weight[0], value_weight[0]]
    joined_kv = jnp.concatenate(local_kv + [to_sibling(part) for part in local_kv], axis=1)
    stack, joined_kv, _ = lax.optimization_barrier((stack, joined_kv, blocks))
    behind, ahead = first_steps(blocks, LAST)
    encoder = exchange(copies(stack, 4), NEAR)
    encoder, behind, ahead = lax.optimization_barrier((encoder, behind, ahead))
    encoder = exchange(spread(encoder, 4), FAR).reshape(X * Y, Z // 2, 2, half, features)
    gathered = last_steps(blocks, behind, ahead, LAST).reshape(dec_rows, width)

    query_halves = local_query.reshape(2, width // 2, cols)
    joined_query = jnp.concatenate(
        [at(query_halves, core), to_sibling(at(query_halves, 1 - core))], axis=1
    )
    out_columns = local_out.T
    row_weight = jnp.concatenate(
        [
            jnp.where(core == 0, local_query, out_columns),
            to_sibling(jnp.where(core == 0, out_columns, local_query)),
        ],
        axis=1,
    )

    made = jnp.dot(gathered, row_weight, preferred_element_type=jnp.float32).astype(jnp.bfloat16)
    made_own, made_other = made[:, :cols], to_sibling(made[:, cols:])
    query_rows = jnp.where(core == 0, made_own, made_other)
    grad_attended = jnp.where(core == 0, made_other, made_own)
    by_place = (4, 4, 2 * rows, -1)

    def swapped(values):
        shape = values.shape
        return values.reshape(by_place).transpose(1, 0, 2, 3).reshape(shape)

    def turned(values, shift):
        return rotated(values.reshape(by_place), shift).reshape(values.shape)

    query_rows = turned(swapped(query_rows), (4 - z_hi) % 4)
    grad_attended = turned(grad_attended, (4 - z_hi) % 4)
    kv_own, kv_sibling = project(strides, encoder, joined_kv)
    attended, grad_query, grad_kv_own, grad_kv_other = attention(
        head_scale, query_rows, grad_attended, kv_own, to_sibling(kv_sibling)
    )

    grad_kv_received = to_sibling(grad_kv_other)
    attended, grad_query = turned(attended, z_hi), swapped(turned(grad_query, z_hi))
    terms = encoder_terms(strides, grad_kv_own, grad_kv_received, joined_kv)
    query_joined = jnp.concatenate([grad_query, to_sibling(grad_query)], axis=1)
    query_joined = jnp.where(core == 0, query_joined, swapped(query_joined))
    terms, encoder, gathered, grad_query, query_joined = lax.optimization_barrier(
        (terms, encoder, gathered, grad_query, query_joined)
    )
    arrived = exchange(terms.reshape(4, 4, Z, half, features), FAR)

    others = to_sibling(gathered)
    normed_all = jnp.where(core == 0, gathered, others)
    cotangent = jnp.where(core == 0, others, gathered)
    out_weight_grad = product(attended, cotangent, ROWS_BY_ROWS).astype(jnp.bfloat16)
    query_weight_grad = product(normed_all, grad_query, ROWS_BY_ROWS).astype(jnp.bfloat16)
    key_weight_grad, value_weight_grad = weight_grads(
        strides, encoder, to_sibling(encoder), grad_kv_own, grad_kv_other
    )

    partial = product(query_joined, joined_query, COLS_BY_COLS).astype(jnp.bfloat16)
    partial = partial.reshape(Z // 2, Y, 2 * rows, width // 2)
    grads = (query_weight_grad, key_weight_grad, value_weight_grad, out_weight_grad)
    total, grads = scatter_ring(partial, LAST, grads)
    arrived, grads = lax.optimization_barrier((arrived, grads))
    query_weight_grad, key_weight_grad, value_weight_grad, out_weight_grad = grads
    total = total.astype(jnp.bfloat16)
    received = [step(total[k], FIRST, k) for k in range(1, Y)]
    arrived = exchange(add(arrived).astype(jnp.bfloat16), NEAR)
    arrived = lax.all_to_all(add(arrived).astype(jnp.bfloat16), z_axes, 0, 0, tiled=True)
    arrived, received = lax.optimization_barrier((arrived, received))
    total = add(total[0], *received)
    final = add(arrived)
    final = final.astype(jnp.bfloat16).reshape(half, 2, tokens).transpose(1, 0, 2)
    encoder_grad = ordered(
        at(final, core), to_sibling(at(final, 1 - core)), core
    ).reshape(tokens, tokens)

    total = total.reshape(2, rows, width // 2)
    grad_normed = jnp.concatenate(
        list(ordered(at(total, core), to_sibling(at(total, 1 - core)), core)), axis=1
    )
    decoder_grad = (
        (grad_normed - normed_full * jnp.mean(grad_normed * normed_full, axis=-1, keepdims=True))
        * inv_rms
    ).astype(jnp.bfloat16)

    return (
        encoder_grad,
        decoder_grad[None],
        query_weight_grad[None],
        key_weight_grad[None],
        value_weight_grad[None],
        out_weight_grad[None],
    )


def solution(mesh):
    section, tensor = AXES[:2], AXES[2:]
    placed = (
        P(section, tensor),
        P(section, tensor, None),
        P(section, tensor, None),
        P(section, None, tensor),
        P(section, None, tensor),
        P(section, None, tensor),
        P(section, tensor, None),
        P(section, tensor),
    )
    return jax.shard_map(
        per_device,
        mesh=Mesh(mesh.devices.reshape(X, 2, Z // 2, Y, CORES), AXES),
        in_specs=placed,
        out_specs=placed[:2] + placed[3:7],
        check_vma=False,
    )
```
